32 devices in a mesh: grp: 2 (over x), seq: 16 (over z, y, core).
Axes of the slice: x: 2, y: 2, z: 4, core: 2. Of those that a mesh axis runs over, the one named last changes fastest.
Arguments:
- signal: bfloat16 [32768, 768], P(('grp', 'seq')), parts along dimension 0, may hold values from -6 to 6
- dilated_tap_weight: bfloat16 [4, 3, 768, 384], replicated, may hold values from -0.125 to 0.125
- point_weight: bfloat16 [4, 384, 768], replicated, may hold values from -0.3125 to 0.3125
Outputs:
- activations: bfloat16 [4, 32768, 768], P(None, ('grp', 'seq')), parts along dimension 1
The draws below stay inside these ranges and needn't reach their ends.
There are 2 independent parts, one for each index of `grp`. The reference program is written for one: setup_inputs(seed, part) draws one part's arguments, and reference() takes and returns one part's arrays. A program takes and returns all parts, laid end to end along the dimension named above; an argument that names none is the same for every part. Nothing has to cross between parts.
All inputs are finite; a program needn't handle non-finite values.
Results may differ from the reference program's by a relative error of at most 0.0075.
Values may be sent and summed in bfloat16 or wider, within the bound.
A program may use at most 64 MiB of HBM per device.

```python
import jax
import jax.numpy as jnp
from jax import lax

C = 768
H = 384
FIRST_DILATION = 256
BLOCKS = 4
BINS = 16384


def block_scale(stream_key, dims, pieces, smallest, top_value):
    gain = 1.0
    for axis_at, shards_of in pieces:
        heights = jax.random.uniform(jax.random.fold_in(jax.random.fold_in(stream_key, 6), axis_at), (shards_of,), jnp.float32, smallest / len(pieces), top_value / len(pieces))
        gain = gain * jnp.repeat(jnp.exp(heights), dims[axis_at] // shards_of).reshape((-1,) + (1,) * (len(dims) - 1 - axis_at))
    return gain


def noise(rng, shape, width, bound, shards=(), held_as=jnp.bfloat16):
    loudness = block_scale(rng, shape, shards, -0.22, 0.18) if shards else 1.0
    entries = jax.random.normal(rng, shape, jnp.float32) * width * loudness
    return jnp.minimum(jnp.maximum(entries, -bound), bound).astype(held_as)


def setup_inputs(seed: int = 0, part: int = 0) -> dict:
    seeds = jax.random.split(jax.random.key(seed), 4)
    part_keys = jax.random.split(jax.random.fold_in(seeds[3], part), 4)
    return {
        "signal": noise(part_keys[0], (BINS, C), 1.0, 6.0, ((0, 16),)),
        "dilated_tap_weight": noise(seeds[1], (BLOCKS, 3, C, H), (3 * C) ** -0.5, 0.125),
        "point_weight": noise(seeds[2], (BLOCKS, H, C), H ** -0.5, 0.3125),
    }


def tap_term(rows, weight):
    product = jnp.dot(rows, weight, preferred_element_type=jnp.float32).astype(jnp.bfloat16)
    return lax.optimization_barrier(product).astype(jnp.float32)


def reference(signal, dilated_tap_weight, point_weight):
    current = signal
    outputs = []
    for block_layer_index in range(BLOCKS):
        dilation_step = FIRST_DILATION * 2 ** block_layer_index
        lower_neighbour_rows = jnp.pad(current, ((dilation_step, 0), (0, 0)))[:BINS]
        above_side = jnp.pad(current, ((0, dilation_step), (0, 0)))[dilation_step:]
        convolved = jnp.dot(current, dilated_tap_weight[block_layer_index, 1], preferred_element_type=jnp.float32)
        convolved = convolved + tap_term(lower_neighbour_rows, dilated_tap_weight[block_layer_index, 0])
        convolved = convolved + tap_term(above_side, dilated_tap_weight[block_layer_index, 2])
        hidden = jax.nn.gelu(convolved, approximate=True).astype(jnp.bfloat16)
        residual_branch = jnp.dot(hidden, point_weight[block_layer_index], preferred_element_type=jnp.float32)
        current = (current.astype(jnp.float32) + residual_branch).astype(jnp.bfloat16)
        outputs.append(current)
    return jnp.stack(outputs)
```

```python
import functools

import jax
import jax.numpy as jnp
from jax import lax
from jax.experimental import pallas as pl
from jax.experimental.pallas import tpu as pltpu
from jax.sharding import PartitionSpec as P

FIRST_DILATION = 256
MESH = pl.DeviceIdType.MESH


def edges_first(count):
    order = []
    for i in range((count + 1) // 2):
        order.append(i)
        if count - 1 - i != i:
            order.append(count - 1 - i)
    return order


def kernel(n, steps, x_hbm, w_hbm, p_hbm, out_hbm, xs, wv, pv, cen, own, lt, rt, rl, rr,
           send_l, send_r, recv_l, recv_r, sem_x, sem_w, sem_p, sem_o):
    blocks = len(steps)
    chunks, rows = xs.shape[1], xs.shape[2]
    hid = p_hbm.shape[1]
    me = lax.axis_index("seq")

    def relay(b):
        return steps[b] > chunks

    def places(b):
        hop = steps[b] // chunks
        odd = lax.rem(lax.div(me, hop), 2)
        partner = me + hop - 2 * hop * odd
        target = me - 2 * hop + 4 * hop * odd
        source = me + 2 * hop - 4 * hop * odd
        return odd, partner, target, source

    def inside(place):
        return jnp.logical_and(place >= 0, place < n)

    greeted = [me - 1, me + 1]
    for b in range(blocks):
        if relay(b):
            _, partner, target, source = places(b)
            greeted += [partner, target, source]
    barrier = pltpu.get_barrier_semaphore()
    for place in greeted:
        @pl.when(inside(place))
        def _():
            pl.semaphore_signal(barrier, inc=1, device_id={"seq": place}, device_id_type=MESH)

    first = edges_first(chunks)
    def x_load(c):
        return pltpu.make_async_copy(x_hbm.at[pl.ds(c * rows, rows)], xs.at[0, c], sem_x.at[c])

    def w_load(b, t):
        source = t
        if relay(b) and t != 1:
            odd = places(b)[0]
            source = 2 - 2 * odd if t == 0 else 2 * odd
        return pltpu.make_async_copy(
            w_hbm.at[b, source], wv.at[b, :, pl.ds(t * hid, hid)], sem_w.at[b, t])

    def p_load(b):
        return pltpu.make_async_copy(p_hbm.at[b], pv.at[b], sem_p.at[b])

    x_load(first[0]).start()
    for t in range(3):
        w_load(0, t).start()
    for c in first[1:]:
        x_load(c).start()
    p_load(0).start()
    for b in range(1, blocks):
        for t in range(3):
            w_load(b, t).start()
        p_load(b).start()

    @pl.when(me == 0)
    def _():
        for b in range(blocks):
            if not relay(b):
                rl[b] = jnp.zeros(rl.shape[1:], rl.dtype)

    @pl.when(me == n - 1)
    def _():
        for b in range(blocks):
            if not relay(b):
                rr[b] = jnp.zeros(rr.shape[1:], rr.dtype)

    for b in range(blocks):
        if relay(b):
            @pl.when(jnp.logical_not(inside(places(b)[3])))
            def _():
                rl[b] = jnp.zeros(rl.shape[1:], rl.dtype)

    def left_copy(b, s, d, place):
        return pltpu.make_async_remote_copy(
            src_ref=lt.at[b, s], dst_ref=rl.at[b, d], send_sem=send_l.at[b, s],
            recv_sem=recv_l.at[b, d], device_id={"seq": place}, device_id_type=MESH)

    def right_copy(b, s, d, place):
        return pltpu.make_async_remote_copy(
            src_ref=rt.at[b, s], dst_ref=rr.at[b, d], send_sem=send_r.at[b, s],
            recv_sem=recv_r.at[b, d], device_id={"seq": place}, device_id_type=MESH)

    sent = []

    def send(copy, place, guarded):
        if not guarded:
            copy.start()
            sent.append((copy, None))
            return

        @pl.when(inside(place))
        def _():
            copy.start()
        sent.append((copy, place))

    def taps(b, c):
        if b == 0:
            x_load(c).wait()
        if taps_done[b] == 0:
            for t in range(3):
                w_load(b, t).wait()
        taps_done[b] += 1
        y = jnp.dot(xs[b, c], wv[b], preferred_element_type=jnp.float32)
        lt[b, c] = y[:, :hid].astype(lt.dtype)
        cen[c] = y[:, hid:2 * hid]
        if relay(b):
            own[c] = y[:, 2 * hid:]
        else:
            rt[b, c] = y[:, 2 * hid:].astype(rt.dtype)
        if b == 0 and taps_done[b] == 1:
            peers = sum(inside(place).astype(jnp.int32) for place in greeted)
            pl.semaphore_wait(barrier, peers)
        if relay(b):
            target = places(b)[2]
            send(left_copy(b, c, c, target), target, True)
            return
        step = steps[b]
        if c + step >= chunks:
            send(left_copy(b, c, c + step - chunks, me + 1), me + 1, True)
        if c < step:
            send(right_copy(b, c, c - step + chunks, me - 1), me - 1, True)

    def pass_on(b, c):
        _, partner, target, source = places(b)

        @pl.when(inside(source))
        def _():
            left_copy(b, c, c, target).wait_recv()
        rt[b, c] = (own[c] + rl[b, c].astype(jnp.float32)).astype(rt.dtype)
        send(right_copy(b, c, c, partner), partner, False)

    def mix(b, c):
        v = cen[c]
        if relay(b):
            right_copy(b, c, c, places(b)[1]).wait_recv()
            v = v + rr[b, c].astype(jnp.float32)
        else:
            step = steps[b]
            if c >= step:
                v = v + lt[b, c - step].astype(jnp.float32)
            else:
                @pl.when(me > 0)
                def _():
                    left_copy(b, c - step + chunks, c, me + 1).wait_recv()
                v = v + rl[b, c].astype(jnp.float32)
            if c + step < chunks:
                v = v + rt[b, c + step].astype(jnp.float32)
            else:
                @pl.when(me < n - 1)
                def _():
                    right_copy(b, c + step - chunks, c, me - 1).wait_recv()
                v = v + rr[b, c].astype(jnp.float32)
        if mix_done[b] == 0:
            p_load(b).wait()
        mix_done[b] += 1
        hidden = jax.nn.gelu(v, approximate=True).astype(jnp.bfloat16)
        branch = jnp.dot(hidden, pv[b], preferred_element_type=jnp.float32)
        xs[b + 1, c] = (xs[b, c].astype(jnp.float32) + branch).astype(xs.dtype)
        out_copy(b, c).start()

    def out_copy(b, c):
        return pltpu.make_async_copy(
            xs.at[b + 1, c], out_hbm.at[b, pl.ds(c * rows, rows)], sem_o.at[b, c])

    taps_done = [0] * blocks
    mix_done = [0] * blocks
    unpassed = []
    for c in first:
        taps(0, c)
    for b in range(blocks):
        order = first
        if steps[b] < chunks:
            order = sorted(first, key=lambda c: (c < steps[b]) + (c + steps[b] >= chunks))
        for i, c in enumerate(order):
            mix(b, c)
            if relay(b) and unpassed:
                pass_on(b, unpassed.pop(0))
            if b + 1 < blocks:
                taps(b + 1, c)
                if relay(b + 1):
                    if i:
                        pass_on(b + 1, unpassed.pop(0))
                    unpassed.append(c)

    for copy, place in sent:
        if place is None:
            copy.wait_send()
        else:
            @pl.when(inside(place))
            def _():
                copy.wait_send()
    for b in range(blocks):
        for c in range(chunks):
            out_copy(b, c).wait()


def shards(n, signal, dilated_tap_weight, point_weight):
    length, wide = signal.shape
    blocks, taps, _, hid = dilated_tap_weight.shape
    rows = min(FIRST_DILATION, length)
    chunks = length // rows
    steps = [FIRST_DILATION * 2**b // rows for b in range(blocks)]
    for step in steps:
        hop = step // chunks
        assert step <= chunks or (step % chunks == 0 and n % (2 * hop) == 0)
    bf16, f32 = jnp.bfloat16, jnp.float32
    terms = pltpu.VMEM((blocks, chunks, rows, hid), bf16)
    dma = pltpu.SemaphoreType.DMA
    return pl.pallas_call(
        functools.partial(kernel, n, steps),
        out_shape=jax.ShapeDtypeStruct((blocks, length, wide), bf16),
        in_specs=[pl.BlockSpec(memory_space=pl.ANY)] * 3,
        out_specs=pl.BlockSpec(memory_space=pl.ANY),
        scratch_shapes=[
            pltpu.VMEM((blocks + 1, chunks, rows, wide), bf16),
            pltpu.VMEM((blocks, wide, taps * hid), bf16),
            pltpu.VMEM((blocks, hid, wide), bf16),
            pltpu.VMEM((chunks, rows, hid), f32),
            pltpu.VMEM((chunks, rows, hid), f32),
            terms, terms, terms, terms,
            dma((blocks, chunks)), dma((blocks, chunks)),
            dma((blocks, chunks)), dma((blocks, chunks)),
            dma((chunks,)), dma((blocks, taps)), dma((blocks,)), dma((blocks, chunks)),
        ],
        compiler_params=pltpu.CompilerParams(
            collective_id=0, has_side_effects=True, vmem_limit_bytes=56 * 2**20),
    )(signal, dilated_tap_weight, point_weight)


def solution(mesh):
    in_specs = (P(("grp", "seq"), None), P(), P())
    out_specs = P(None, ("grp", "seq"), None)
    return jax.shard_map(functools.partial(shards, mesh.shape["seq"]), mesh=mesh,
                         in_specs=in_specs, out_specs=out_specs, check_vma=False)
```

```python
import functools

import jax
import jax.numpy as jnp
from jax import lax
from jax.experimental import pallas as pl
from jax.experimental.pallas import tpu as pltpu
from jax.sharding import PartitionSpec as P

FIRST_DILATION = 256
MESH = pl.DeviceIdType.MESH


def edges_first(count):
    order = []
    for i in range((count + 1) // 2):
        order.append(i)
        if count - 1 - i != i:
            order.append(count - 1 - i)
    return order


def kernel(n, steps, x_hbm, w_hbm, p_hbm, out, xs, wv, pv, cen, own, to, ti, ro, ri,
           send_o, send_i, recv_o, recv_i, sem_x, sem_w, sem_p):
    blocks = len(steps)
    chunks, rows = xs.shape[0], xs.shape[1]
    hid = p_hbm.shape[1]
    me = lax.axis_index("seq")
    core = lax.rem(me, 2)
    outer = me - 1 + 2 * core
    inner = me + 1 - 2 * core

    def relay(b):
        return steps[b] > chunks

    def places(b):
        hop = steps[b] // chunks
        odd = lax.rem(lax.div(me, hop), 2)
        partner = me + hop - 2 * hop * odd
        target = me - 2 * hop + 4 * hop * odd
        source = me + 2 * hop - 4 * hop * odd
        return odd, partner, target, source

    def inside(place):
        return jnp.logical_and(place >= 0, place < n)

    greeted = [outer, inner]
    for b in range(blocks):
        if relay(b):
            _, partner, target, source = places(b)
            greeted += [partner, target, source]
    barrier = pltpu.get_barrier_semaphore()
    for place in greeted:
        @pl.when(inside(place))
        def _():
            pl.semaphore_signal(barrier, inc=1, device_id={"seq": place}, device_id_type=MESH)

    def span(c):
        at = (c + core * (chunks - 1 - 2 * c)) * rows
        return pl.ds(pl.multiple_of(at, rows), rows)

    def x_load(c):
        return pltpu.make_async_copy(x_hbm.at[span(c)], xs.at[c], sem_x.at[c])

    def w_load(b, t):
        side = places(b)[0] if relay(b) else core
        source = (2 - 2 * side, 1, 2 * side)[t]
        return pltpu.make_async_copy(
            w_hbm.at[b, source], wv.at[b, :, pl.ds(t * hid, hid)], sem_w.at[b, t])

    def p_load(b):
        return pltpu.make_async_copy(p_hbm.at[b], pv.at[b], sem_p.at[b])

    x_load(0).start()
    for t in range(3):
        w_load(0, t).start()
    for c in range(1, chunks):
        x_load(c).start()
    p_load(0).start()
    for b in range(1, blocks):
        for t in range(3):
            w_load(b, t).start()
        p_load(b).start()

    def fill_ends():
        for b in range(blocks):
            source = places(b)[3] if relay(b) else outer

            @pl.when(jnp.logical_not(inside(source)))
            def _():
                for c in range(min(steps[b], chunks)):
                    ro[b, c] = jnp.zeros(ro.shape[2:], ro.dtype)

    def outer_copy(b, s, d, place):
        return pltpu.make_async_remote_copy(
            src_ref=to.at[b, s], dst_ref=ro.at[b, d], send_sem=send_o.at[b, s],
            recv_sem=recv_o.at[b, d], device_id={"seq": place}, device_id_type=MESH)

    def inner_copy(b, s, d, place):
        return pltpu.make_async_remote_copy(
            src_ref=ti.at[b, s], dst_ref=ri.at[b, d], send_sem=send_i.at[b, s],
            recv_sem=recv_i.at[b, d], device_id={"seq": place}, device_id_type=MESH)

    sent = []

    def send(copy, place=None):
        if place is None:
            copy.start()
        else:
            @pl.when(inside(place))
            def _():
                copy.start()
        sent.append((copy, place))

    def x_of(b, c):
        return xs[c] if b == 0 else out[b - 1, span(c), :]

    def send_outer(b, c):
        if relay(b):
            target = places(b)[2]
            send(outer_copy(b, c, c, target), target)
        elif c < steps[b]:
            send(outer_copy(b, c, steps[b] - 1 - c, outer), outer)

    loaded = set()

    def once(load, *key):
        if (load, key) not in loaded:
            loaded.add((load, key))
            load(*key).wait()

    def taps(b, c):
        if b == 0:
            x_load(c).wait()
        x = x_of(b, c)
        once(w_load, b, 0)
        opening = b == 0 and c == 0
        if opening:
            y = jnp.dot(x, wv[b, :, :hid], preferred_element_type=jnp.float32)
            to[b, c] = y.astype(to.dtype)
            peers = sum(inside(place).astype(jnp.int32) for place in greeted)
            pl.semaphore_wait(barrier, peers)
            send_outer(b, c)
            fill_ends()
        once(w_load, b, 1)
        once(w_load, b, 2)
        if opening:
            y = jnp.dot(x, wv[b, :, hid:], preferred_element_type=jnp.float32)
        else:
            y = jnp.dot(x, wv[b], preferred_element_type=jnp.float32)
            to[b, c] = y[:, :hid].astype(to.dtype)
            send_outer(b, c)
            y = y[:, hid:]
        cen[c] = y[:, :hid]
        if relay(b):
            own[c] = y[:, hid:]
            return
        ti[b, c] = y[:, hid:].astype(ti.dtype)
        if c + steps[b] >= chunks:
            send(inner_copy(b, c, 2 * chunks - 1 - c - steps[b], inner))

    def pass_on(b, c):
        _, partner, target, source = places(b)

        @pl.when(inside(source))
        def _():
            outer_copy(b, c, c, target).wait_recv()
        ti[b, c] = (own[c] + ro[b, c].astype(jnp.float32)).astype(ti.dtype)
        send(inner_copy(b, c, c, partner))

    def mix(b, c):
        v = cen[c]
        step = steps[b]
        if relay(b):
            inner_copy(b, c, c, places(b)[1]).wait_recv()
            v = v + ri[b, c].astype(jnp.float32)
        else:
            if c + step < chunks:
                v = v + to[b, c + step].astype(jnp.float32)
            else:
                inner_copy(b, 2 * chunks - 1 - c - step, c, inner).wait_recv()
                v = v + ri[b, c].astype(jnp.float32)
            if c >= step:
                v = v + ti[b, c - step].astype(jnp.float32)
            else:
                @pl.when(inside(outer))
                def _():
                    outer_copy(b, step - 1 - c, c, outer).wait_recv()
                v = v + ro[b, c].astype(jnp.float32)
        once(p_load, b)
        hidden = jax.nn.gelu(v, approximate=True).astype(jnp.bfloat16)
        branch = jnp.dot(hidden, pv[b], preferred_element_type=jnp.float32)
        out[b, span(c), :] = (x_of(b, c).astype(jnp.float32) + branch).astype(out.dtype)

    for kind, b, c in plan(steps, chunks):
        {"taps": taps, "mix": mix, "pass": pass_on}[kind](b, c)

    for copy, place in sent:
        if place is None:
            copy.wait_send()
        else:
            @pl.when(inside(place))
            def _():
                copy.wait_send()


def plan(steps, chunks):
    blocks = len(steps)
    when = {("taps", 0, c): 0.0 for c in range(chunks)}
    done, order, clock = {}, [], 0.0
    wire = {"off": 0.0, "on": 0.0}
    jobs = [("taps", b, c) for b in range(blocks) for c in range(chunks)]
    jobs += [("mix", b, c) for b in range(blocks) for c in range(chunks)]
    jobs += [("pass", b, c) for b in range(blocks) for c in range(chunks) if steps[b] > chunks]
    arrive = {}

    def needs(job):
        kind, b, c = job
        step = steps[b]
        if kind == "taps":
            return [done.get(("mix", b - 1, c))] if b else [0.0]
        if kind == "pass":
            return [done.get(("taps", b, c)), arrive.get(("off", b, c))]
        if step > chunks:
            return [done.get(("taps", b, c)), arrive.get(("on", b, c))]
        got = [done.get(("taps", b, c))]
        got.append(done.get(("taps", b, c + step)) if c + step < chunks else arrive.get(("on", b, c)))
        got.append(done.get(("taps", b, c - step)) if c >= step else arrive.get(("off", b, c)))
        return got

    while jobs:
        best = None
        for job in jobs:
            got = needs(job)
            if None in got:
                continue
            start = max([clock] + got)
            kind, b, c = job
            key = (start, {"pass": 0, "taps": 1, "mix": 2}[kind] if b else 3, c if b == 0 else 0)
            if kind == "mix":
                outward = b + 1 < blocks and c < steps[b + 1]
                key = (start, 2 if outward else 4, c)
            if best is None or key < best[0]:
                best = (key, job)
        (start, *_), job = best
        kind, b, c = job
        step = steps[b]
        jobs.remove(job)
        order.append(job)
        clock = start + {"taps": 0.7, "mix": 0.4, "pass": 0.1}[kind]
        done[job] = clock

        def fly(way, d, cost):
            wire[way] = max(wire[way], clock) + cost
            arrive[(way, b, d)] = wire[way] + 1.5
        if kind == "pass":
            wire["off"] = max(wire["off"], clock) + 4.0
            arrive[("on", b, c)] = wire["off"] + 1.5
        elif kind == "taps" and step > chunks:
            arrive[("off", b, c)] = clock + 6.0
        elif kind == "taps":
            if c < step:
                fly("off", step - 1 - c, 4.0)
            if c + step >= chunks:
                fly("on", 2 * chunks - 1 - c - step, 0.5)
    return order


def shards(n, signal, dilated_tap_weight, point_weight):
    length, wide = signal.shape
    blocks, taps, _, hid = dilated_tap_weight.shape
    rows = min(FIRST_DILATION, length)
    chunks = length // rows
    steps = [FIRST_DILATION * 2**b // rows for b in range(blocks)]
    assert n % 2 == 0
    for step in steps:
        hop = step // chunks
        assert step <= chunks or (step % chunks == 0 and n % (2 * hop) == 0)
    bf16, f32 = jnp.bfloat16, jnp.float32
    terms = pltpu.VMEM((blocks, chunks, rows, hid), bf16)
    dma = pltpu.SemaphoreType.DMA
    return pl.pallas_call(
        functools.partial(kernel, n, steps),
        out_shape=pltpu.VMEM((blocks, length, wide), bf16),
        in_specs=[pl.BlockSpec(memory_space=pl.ANY)] * 3,
        out_specs=pl.BlockSpec(memory_space=pltpu.VMEM),
        scratch_shapes=[
            pltpu.VMEM((chunks, rows, wide), bf16),
            pltpu.VMEM((blocks, wide, taps * hid), bf16),
            pltpu.VMEM((blocks, hid, wide), bf16),
            pltpu.VMEM((chunks, rows, hid), f32),
            pltpu.VMEM((chunks, rows, hid), f32),
            terms, terms, terms, terms,
            dma((blocks, chunks)), dma((blocks, chunks)),
            dma((blocks, chunks)), dma((blocks, chunks)),
            dma((chunks,)), dma((blocks, taps)), dma((blocks,)),
        ],
        compiler_params=pltpu.CompilerParams(
            collective_id=0, has_side_effects=True, vmem_limit_bytes=48 * 2**20),
    )(signal, dilated_tap_weight, point_weight)


def solution(mesh):
    in_specs = (P(("grp", "seq"), None), P(), P())
    out_specs = P(None, ("grp", "seq"), None)
    return jax.shard_map(functools.partial(shards, mesh.shape["seq"]), mesh=mesh,
                         in_specs=in_specs, out_specs=out_specs, check_vma=False)
```

```python
import functools

import jax
import jax.numpy as jnp
from jax import lax
from jax.experimental import pallas as pl
from jax.experimental.pallas import tpu as pltpu
from jax.sharding import PartitionSpec as P

FIRST_DILATION = 256
MESH = pl.DeviceIdType.MESH


def edges_first(count):
    order = []
    for i in range((count + 1) // 2):
        order.append(i)
        if count - 1 - i != i:
            order.append(count - 1 - i)
    return order


def kernel(n, steps, x_hbm, w_hbm, p_hbm, out, xs, wv, pv, cen, own, to, ti, ro, ri, held,
           send_o, send_i, recv_o, recv_i, sem_x, sem_w, sem_p, send_h, recv_h):
    blocks = len(steps)
    chunks, rows = xs.shape[0], xs.shape[1]
    hid = p_hbm.shape[1]
    me = lax.axis_index("seq")
    core = lax.rem(me, 2)
    outer = me - 1 + 2 * core
    inner = me + 1 - 2 * core

    def relay(b):
        return steps[b] > chunks

    def places(b):
        hop = steps[b] // chunks
        odd = lax.rem(lax.div(me, hop), 2)
        partner = me + hop - 2 * hop * odd
        target = me - 2 * hop + 4 * hop * odd
        source = me + 2 * hop - 4 * hop * odd
        return odd, partner, target, source

    def inside(place):
        return jnp.logical_and(place >= 0, place < n)

    greeted = [outer, inner]
    for b in range(blocks):
        if relay(b):
            _, partner, target, source = places(b)
            greeted += [partner, target, source]
    order = plan(steps, chunks)

    side = lax.rem(lax.div(me, 2), 2)
    beside = me + 2 - 4 * side
    beyond = me - 3 + 6 * core
    quads = n // 4
    along = lax.div(me, 4)
    along = along + core * (quads - 1 - 2 * along)
    share = lax.div(along * chunks, quads)
    if any(detour(steps, chunks, b) for b in range(blocks)):
        greeted.append(beyond)

    def detoured(b, c):
        turn = [k for kind, at, k in order if kind == "taps" and at == b].index(c)
        rank = (chunks - 2, *range(chunks - 2), chunks - 1)[turn]
        return rank < share

    barrier = pltpu.get_barrier_semaphore()
    for place in greeted:
        @pl.when(inside(place))
        def _():
            pl.semaphore_signal(barrier, inc=1, device_id={"seq": place}, device_id_type=MESH)

    def span(c):
        at = (c + core * (chunks - 1 - 2 * c)) * rows
        return pl.ds(pl.multiple_of(at, rows), rows)

    def x_load(c):
        return pltpu.make_async_copy(x_hbm.at[span(c)], xs.at[c], sem_x.at[c])

    def w_load(b, t):
        side = places(b)[0] if relay(b) else core
        source = (2 - 2 * side, 1, 2 * side)[t]
        return pltpu.make_async_copy(
            w_hbm.at[b, source], wv.at[b, :, pl.ds(t * hid, hid)], sem_w.at[b, t])

    def p_load(b):
        return pltpu.make_async_copy(p_hbm.at[b], pv.at[b], sem_p.at[b])

    x_load(0).start()
    for t in range(3):
        w_load(0, t).start()

    def load_block():
        for c in range(1, chunks):
            x_load(c).start()
        p_load(0).start()

    def load_rest():
        for b in range(1, blocks):
            for t in range(3):
                w_load(b, t).start()
            p_load(b).start()

    def fill_ends():
        for b in range(blocks):
            source = places(b)[3] if relay(b) else outer

            @pl.when(jnp.logical_not(inside(source)))
            def _():
                for c in range(min(steps[b], chunks)):
                    ro[b, c] = jnp.zeros(ro.shape[2:], ro.dtype)

    def outer_copy(b, s, d, place):
        return pltpu.make_async_remote_copy(
            src_ref=to.at[b, s], dst_ref=ro.at[b, d], send_sem=send_o.at[b, s],
            recv_sem=recv_o.at[b, d], device_id={"seq": place}, device_id_type=MESH)

    def inner_copy(b, s, d, place):
        return pltpu.make_async_remote_copy(
            src_ref=ti.at[b, s], dst_ref=ri.at[b, d], send_sem=send_i.at[b, s],
            recv_sem=recv_i.at[b, d], device_id={"seq": place}, device_id_type=MESH)

    def aside_copy(b, c):
        return pltpu.make_async_remote_copy(
            src_ref=to.at[b, c], dst_ref=held.at[c], send_sem=send_o.at[b, c],
            recv_sem=recv_h.at[c], device_id={"seq": beside}, device_id_type=MESH)

    def onward_copy(b, c):
        return pltpu.make_async_remote_copy(
            src_ref=held.at[c], dst_ref=ro.at[b, steps[b] - 1 - c], send_sem=send_h.at[c],
            recv_sem=recv_o.at[b, steps[b] - 1 - c], device_id={"seq": beyond}, device_id_type=MESH)

    def hand_on(b, c):
        @pl.when(jnp.logical_and(side != core, detoured(b, c)))
        def _():
            aside_copy(b, c).wait_recv()
            onward_copy(b, c).start()

    sent = []

    def send(copy, place=None):
        if place is None:
            copy.start()
        else:
            @pl.when(inside(place))
            def _():
                copy.start()
        sent.append((copy, place))

    def x_of(b, c):
        return xs[c] if b == 0 else out[b - 1, span(c), :]

    def send_outer(b, c):
        if relay(b):
            target = places(b)[2]
            send(outer_copy(b, c, c, target), target)
        elif detour(steps, chunks, b):
            around = jnp.logical_and(side == core, detoured(b, c))
            straight = outer_copy(b, c, steps[b] - 1 - c, outer)

            @pl.when(around)
            def _():
                aside_copy(b, c).start()

            @pl.when(jnp.logical_and(inside(outer), jnp.logical_not(around)))
            def _():
                straight.start()
            sent.append((straight, outer))
        elif c < steps[b]:
            send(outer_copy(b, c, steps[b] - 1 - c, outer), outer)

    loaded = set()

    def once(load, *key):
        if (load, key) not in loaded:
            loaded.add((load, key))
            load(*key).wait()

    def taps(b, c):
        if b == 0:
            x_load(c).wait()
        x = x_of(b, c)
        once(w_load, b, 0)
        opening = b == 0 and c == 0
        if opening:
            load_block()
            y = jnp.dot(x, wv[b, :, :hid], preferred_element_type=jnp.float32)
            to[b, c] = y.astype(to.dtype)
            peers = sum(inside(place).astype(jnp.int32) for place in greeted)
            pl.semaphore_wait(barrier, peers)
            send_outer(b, c)
            fill_ends()
            load_rest()
        once(w_load, b, 1)
        once(w_load, b, 2)
        if opening:
            y = jnp.dot(x, wv[b, :, hid:], preferred_element_type=jnp.float32)
        else:
            y = jnp.dot(x, wv[b], preferred_element_type=jnp.float32)
            to[b, c] = y[:, :hid].astype(to.dtype)
            send_outer(b, c)
            y = y[:, hid:]
        cen[c] = y[:, :hid]
        if relay(b):
            own[c] = y[:, hid:]
            return
        ti[b, c] = y[:, hid:].astype(ti.dtype)
        if c + steps[b] >= chunks:
            send(inner_copy(b, c, 2 * chunks - 1 - c - steps[b], inner))

    def pass_on(b, c):
        _, partner, target, source = places(b)

        @pl.when(inside(source))
        def _():
            outer_copy(b, c, c, target).wait_recv()
        ti[b, c] = (own[c] + ro[b, c].astype(jnp.float32)).astype(ti.dtype)
        send(inner_copy(b, c, c, partner))

    def mix(b, c):
        v = cen[c]
        step = steps[b]
        if relay(b):
            inner_copy(b, c, c, places(b)[1]).wait_recv()
            v = v + ri[b, c].astype(jnp.float32)
        else:
            if c + step < chunks:
                v = v + to[b, c + step].astype(jnp.float32)
            else:
                inner_copy(b, 2 * chunks - 1 - c - step, c, inner).wait_recv()
                v = v + ri[b, c].astype(jnp.float32)
            if c >= step:
                v = v + ti[b, c - step].astype(jnp.float32)
            else:
                @pl.when(inside(outer))
                def _():
                    outer_copy(b, step - 1 - c, c, outer).wait_recv()
                v = v + ro[b, c].astype(jnp.float32)
        once(p_load, b)
        hidden = jax.nn.gelu(v, approximate=True).astype(jnp.bfloat16)
        branch = jnp.dot(hidden, pv[b], preferred_element_type=jnp.float32)
        out[b, span(c), :] = (x_of(b, c).astype(jnp.float32) + branch).astype(out.dtype)

    for kind, b, c in order:
        {"taps": taps, "mix": mix, "pass": pass_on, "hand": hand_on}[kind](b, c)

    for copy, place in sent:
        if place is None:
            copy.wait_send()
        else:
            @pl.when(inside(place))
            def _():
                copy.wait_send()
    for kind, b, c in order:
        if kind == "hand":
            @pl.when(jnp.logical_and(side != core, detoured(b, c)))
            def _():
                onward_copy(b, c).wait_send()


def detour(steps, chunks, b):
    return chunks > 1 and steps[b] == chunks and 2 * chunks in steps


def plan(steps, chunks):
    blocks = len(steps)
    when = {("taps", 0, c): 0.0 for c in range(chunks)}
    done, order, clock = {}, [], 0.0
    wire = {"off": 0.0, "on": 0.0}
    jobs = [("taps", b, c) for b in range(blocks) for c in range(chunks)]
    jobs += [("mix", b, c) for b in range(blocks) for c in range(chunks)]
    jobs += [("pass", b, c) for b in range(blocks) for c in range(chunks) if steps[b] > chunks]
    jobs += [("hand", b, c) for b in range(blocks) for c in range(chunks) if detour(steps, chunks, b)]
    arrive = {}

    def needs(job):
        kind, b, c = job
        step = steps[b]
        if kind == "hand":
            return [arrive.get(("hand", b, c))]
        if kind == "taps":
            return [done.get(("mix", b - 1, c))] if b else [0.0]
        if kind == "pass":
            return [done.get(("taps", b, c)), arrive.get(("off", b, c))]
        if step > chunks:
            return [done.get(("taps", b, c)), arrive.get(("on", b, c))]
        got = [done.get(("taps", b, c))]
        got.append(done.get(("taps", b, c + step)) if c + step < chunks else arrive.get(("on", b, c)))
        got.append(done.get(("taps", b, c - step)) if c >= step else arrive.get(("off", b, c)))
        return got

    while jobs:
        best = None
        for job in jobs:
            got = needs(job)
            if None in got:
                continue
            start = max([clock] + got)
            kind, b, c = job
            key = (start, {"hand": 0, "pass": 0, "taps": 1, "mix": 2}[kind] if b else 3, c if b == 0 else 0)
            if kind == "mix":
                outward = b + 1 < blocks and c < steps[b + 1]
                key = (start, 2 if outward else 4, c)
            if best is None or key < best[0]:
                best = (key, job)
        (start, *_), job = best
        kind, b, c = job
        step = steps[b]
        jobs.remove(job)
        order.append(job)
        clock = start + {"taps": 0.7, "mix": 0.4, "pass": 0.1, "hand": 0.0}[kind]
        done[job] = clock

        def fly(way, d, cost):
            wire[way] = max(wire[way], clock) + cost
            arrive[(way, b, d)] = wire[way] + 1.5
        if kind == "pass":
            wire["off"] = max(wire["off"], clock) + 4.0
            arrive[("on", b, c)] = wire["off"] + 1.5
        elif kind == "taps" and step > chunks:
            arrive[("off", b, c)] = clock + 6.0
        elif kind == "taps":
            if c < step:
                fly("off", step - 1 - c, 4.0)
                if detour(steps, chunks, b):
                    arrive[("hand", b, c)] = max(clock, arrive[("off", b, step - 1 - c)] - 4.0)
            if c + step >= chunks:
                fly("on", 2 * chunks - 1 - c - step, 0.5)
    return order


def shards(n, signal, dilated_tap_weight, point_weight):
    length, wide = signal.shape
    blocks, taps, _, hid = dilated_tap_weight.shape
    rows = min(FIRST_DILATION, length)
    chunks = length // rows
    steps = [FIRST_DILATION * 2**b // rows for b in range(blocks)]
    assert n % 2 == 0
    for step in steps:
        hop = step // chunks
        assert step <= chunks or (step % chunks == 0 and n % (2 * hop) == 0)
    bf16, f32 = jnp.bfloat16, jnp.float32
    terms = pltpu.VMEM((blocks, chunks, rows, hid), bf16)
    dma = pltpu.SemaphoreType.DMA
    return pl.pallas_call(
        functools.partial(kernel, n, steps),
        out_shape=pltpu.VMEM((blocks, length, wide), bf16),
        in_specs=[pl.BlockSpec(memory_space=pl.ANY)] * 3,
        out_specs=pl.BlockSpec(memory_space=pltpu.VMEM),
        scratch_shapes=[
            pltpu.VMEM((chunks, rows, wide), bf16),
            pltpu.VMEM((blocks, wide, taps * hid), bf16),
            pltpu.VMEM((blocks, hid, wide), bf16),
            pltpu.VMEM((chunks, rows, hid), f32),
            pltpu.VMEM((chunks, rows, hid), f32),
            terms, terms, terms, terms,
            pltpu.VMEM((chunks, rows, hid), bf16),
            dma((blocks, chunks)), dma((blocks, chunks)),
            dma((blocks, chunks)), dma((blocks, chunks)),
            dma((chunks,)), dma((blocks, taps)), dma((blocks,)),
            dma((chunks,)), dma((chunks,)),
        ],
        compiler_params=pltpu.CompilerParams(
            collective_id=0, has_side_effects=True, vmem_limit_bytes=48 * 2**20),
    )(signal, dilated_tap_weight, point_weight)


def solution(mesh):
    in_specs = (P(("grp", "seq"), None), P(), P())
    out_specs = P(None, ("grp", "seq"), None)
    return jax.shard_map(functools.partial(shards, mesh.shape["seq"]), mesh=mesh,
                         in_specs=in_specs, out_specs=out_specs, check_vma=False)
```
